32 devices in a mesh: group: 2 (over y), ctx: 4 (over z), dp: 4 (over x, core).
Axes of the slice: x: 2, y: 2, z: 4, core: 2. Of those that a mesh axis runs over, the one named last changes fastest.
Arguments:
- queries: bfloat16 [8, 512, 2048], P(('group', 'dp'), 'ctx'), parts along dimension 0, may hold values from -6 to 6
- keys: bfloat16 [8, 512, 2048], P(('group', 'dp'), 'ctx'), parts along dimension 0, may hold values from -6 to 6
- values: bfloat16 [8, 512, 2048], P(('group', 'dp'), 'ctx'), parts along dimension 0, may hold values from -6 to 6
- grad_normed: bfloat16 [8, 512, 2048], P(('group', 'dp'), 'ctx'), parts along dimension 0, may hold values from -6 to 6
- gain: bfloat16 [2048], replicated, may hold values from 0.5 to 1.5
- doc_ids: int32 [8, 4], P(('group', 'dp'), 'ctx'), parts along dimension 0, may hold values from 0 to 2, never falling along the last dimension, each value on 1 to 2 neighbouring positions
Outputs:
- grad_queries: bfloat16 [8, 512, 2048], P(('group', 'dp'), 'ctx'), parts along dimension 0
- grad_keys: bfloat16 [8, 512, 2048], P(('group', 'dp'), 'ctx'), parts along dimension 0
- grad_values: bfloat16 [8, 512, 2048], P(('group', 'dp'), 'ctx'), parts along dimension 0
- grad_gain: float32 [4096], P(('group', 'dp')), parts along dimension 0
The draws below stay inside these ranges and needn't reach their ends.
There are 2 independent parts, one for each index of `group`. The reference program is written for one: setup_inputs(seed, part) draws one part's arguments, and reference() takes and returns one part's arrays. A program takes and returns all parts, laid end to end along the dimension named above; an argument that names none is the same for every part. Nothing has to cross between parts.
Inputs may be any that keep to these rules, and one draw needn't show every extreme that they name: `doc_ids`: along each sequence the document numbers never fall; every number from 0 to 2 appears, and one document holds exactly 2 spans.
All inputs are finite; a program needn't handle non-finite values.
Results may differ from the reference program's by a relative error of at most 0.0058.
Values sent between devices are 32-bit elements; how exact they have to be, the bound alone decides.
A program may use at most 64 MiB of HBM per device.

```python
import math
import jax
import jax.numpy as jnp
import numpy as np
from jax import lax

HEADS = 16
HEAD_DIM = 128
SPAN = 128
HD = 2048
LENGTH = 512
SEQS = 4
SPANS = 4


def strengthened(values, rng, source, target, blocks, factor):
    def block_of(dim):
        return (jnp.arange(values.shape[dim]) // (values.shape[dim] // blocks)).reshape((-1,) + (1,) * (values.ndim - 1 - dim))

    first = jax.random.permutation(rng, blocks)[block_of(target)]
    other_side = (block_of(target) + blocks // 2) % blocks
    return jnp.where((block_of(source) == first) | (block_of(source) == other_side), factor * values, values)


def block_levels(own_key, dims, pieces, low, high):
    def one(position, blocks):
        draws = jax.random.uniform(jax.random.fold_in(jax.random.fold_in(own_key, 6), position), (blocks,), jnp.float32, low / len(pieces), high / len(pieces))
        return jnp.repeat(jnp.exp(draws), dims[position] // blocks).reshape((-1,) + (1,) * (len(dims) - position - 1))

    factor_of = one(*pieces[0])
    for cut in pieces[1:]:
        factor_of = factor_of * one(*cut)
    return factor_of


def profile(number_of, total, most, slope):
    portions = [(1 << 20) // math.isqrt(grade ** slope) + 1 for grade in range(2, number_of + 1)]
    rest, holding = total - most - (number_of - 1), [1] * (number_of - 1)
    while rest > 0:
        candidates = [i for i in range(number_of - 1) if holding[i] < most]
        whole, budget = sum([portions[i] for i in candidates]), rest
        for i in candidates:
            addition = min(most - holding[i], max(1, budget * portions[i] // whole), rest)
            holding[i] = holding[i] + addition
            rest = rest - addition
    return np.array([most] + holding)


def uneven(key, amount, total, reach, slope):
    if amount == 2:
        one = jax.random.randint(key, (), max(1, total - reach), min(reach, total - 1) + 1)
        return jnp.stack([one, total - one])
    tallies = jnp.asarray(profile(amount, total, reach, slope), jnp.int32)
    twos = (amount - 1) // 2
    source_of, receiver = tallies[1:1 + 2 * twos:2], tallies[2:2 + 2 * twos:2]
    room = jnp.minimum(source_of - 1, reach - receiver)
    moved = jax.random.randint(jax.random.fold_in(key, 1), (twos,), 0, 1 << 20) % (room + 1)
    tallies = tallies.at[1:1 + 2 * twos:2].set(source_of - moved).at[2:2 + 2 * twos:2].set(receiver + moved)
    return tallies[jax.random.permutation(jax.random.fold_in(key, 2), amount)]


def noise(stream_key, dims, deviation, bound, shards=(), dtype=jnp.bfloat16):
    drawn = jax.random.normal(stream_key, dims, jnp.float32) * deviation
    if len(shards) > 0:
        drawn = block_levels(stream_key, dims, shards, -0.22, 0.18) * drawn
    return jnp.clip(drawn, min=-bound, max=bound).astype(dtype)


def heavy_noise(own_key, dims, spread, bound, pieces, heavy, held_as=jnp.bfloat16):
    array = spread * jax.random.normal(own_key, dims, jnp.float32)
    if pieces:
        array = array * block_levels(own_key, dims, pieces, -0.22, 0.18)
    return jnp.clip(strengthened(array, jax.random.fold_in(own_key, 3), *heavy), -bound, bound).astype(held_as)


def setup_inputs(seed: int = 0, part: int = 0) -> dict:
    key_of = jax.random.split(jax.random.key(seed), 7)
    own_keys = jax.random.split(jax.random.fold_in(key_of[6], part), 7)
    queries = noise(own_keys[0], (SEQS, LENGTH, HD), 1.0, 6.0, ((0, 4), (1, 4)))
    keys = noise(own_keys[1], (SEQS, LENGTH, HD), 1.0, 6.0, ((0, 4), (1, 4)))
    values = noise(own_keys[2], (SEQS, LENGTH, HD), 1.0, 6.0, ((0, 4), (1, 4)))
    grad_normed = heavy_noise(own_keys[3], (SEQS, LENGTH, HD), 1.0, 6.0, ((0, 4), (1, 4)), (0, 2, 4, 2.0))
    gain = jnp.clip(1.0 + 0.1 * jax.random.normal(key_of[4], (HD,), jnp.float32), 0.5, 1.5).astype(jnp.bfloat16)
    doc_ids = jax.vmap(lambda own: jnp.searchsorted(jnp.cumsum(uneven(own, 3, SPANS, SPANS // 2, 2)), jnp.arange(SPANS), side="right"))(jax.random.split(own_keys[5], SEQS)).reshape((SEQS, SPANS)).astype(jnp.int32)
    return {"queries": queries, "keys": keys, "values": values, "grad_normed": grad_normed, "gain": gain, "doc_ids": doc_ids}


def linked_sum(terms, tags, reverse):

    def advance(carry, item):
        state, last = carry
        term, tag = item
        enter = jnp.where(tag == last, state, jnp.zeros_like(state))
        return ((enter + term, tag), enter)
    start = (jnp.zeros(terms.shape[1:], jnp.float32), jnp.float32(0.0))
    _, entering = lax.scan(advance, start, (terms, tags), reverse=reverse)
    return entering

def round_keep(value):
    return lax.optimization_barrier(value.astype(jnp.bfloat16)).astype(jnp.float32)

def mix(form, left, right):
    return jnp.einsum(form, left, right, precision=lax.Precision.HIGHEST)

def reference(queries, keys, values, grad_normed, gain, doc_ids):
    gain32 = gain.astype(jnp.float32)
    causal = jnp.tril(jnp.ones((SPAN, SPAN), jnp.bool_))

    def one_sequence(items):
        qrow, krow, vrow, grow, drow = items
        count = qrow.shape[0] // SPAN
        shape = (count, SPAN, HEADS, HEAD_DIM)
        qf = qrow.astype(jnp.float32).reshape(shape)
        kf = krow.astype(jnp.float32).reshape(shape)
        vf = vrow.astype(jnp.float32).reshape(shape)
        tags = (drow + 1).astype(jnp.float32)
        scores = mix('cthd,cshd->chts', qf, kf)
        intra = round_keep(jnp.where(causal, scores, 0.0))
        kv_terms = mix('cthd,cthe->chde', kf, vf)
        state_b = round_keep(linked_sum(kv_terms, tags, False))
        attn = mix('chts,cshe->cthe', intra, vf) + mix('cthd,chde->cthe', qf, state_b)
        attn = attn.reshape(qrow.shape)
        inv = 1.0 / jnp.sqrt(lax.optimization_barrier(jnp.mean(attn * attn, axis=-1, keepdims=True)) + 1e-05)
        gradf = grow.astype(jnp.float32)
        gain_term = lax.optimization_barrier(jnp.sum(gradf * attn * inv, axis=0))
        upper = gradf * gain32
        inner = lax.optimization_barrier(jnp.sum(upper * attn, axis=-1, keepdims=True))
        grad_attn = round_keep(upper * inv - attn * inner * inv ** 3 / HD).reshape(shape)
        grad_intra = round_keep(jnp.where(causal, mix('cthe,cshe->chts', grad_attn, vf), 0.0))
        qdo_terms = mix('cthd,cthe->chde', qf, grad_attn)
        back_b = round_keep(linked_sum(qdo_terms, tags, True))
        grad_q = mix('chts,cshd->cthd', grad_intra, kf) + mix('cthe,chde->cthd', grad_attn, state_b)
        grad_k = mix('chts,cthd->cshd', grad_intra, qf) + mix('cshe,chde->cshd', vf, back_b)
        grad_v = mix('chts,cthe->cshe', intra, grad_attn) + mix('cshd,chde->cshe', kf, back_b)
        flat = qrow.shape
        return (grad_q.reshape(flat).astype(jnp.bfloat16), grad_k.reshape(flat).astype(jnp.bfloat16), grad_v.reshape(flat).astype(jnp.bfloat16), gain_term)
    grad_q, grad_k, grad_v, gain_terms = lax.map(one_sequence, (queries, keys, values, grad_normed, doc_ids))
    return (grad_q, grad_k, grad_v, lax.optimization_barrier(jnp.sum(gain_terms, axis=0)))
```

```python
import functools

import jax
import jax.numpy as jnp
from jax import lax
from jax.experimental import pallas as pl
from jax.experimental.pallas import tpu as pltpu
from jax.sharding import PartitionSpec as P

HEADS = 16
DIM = 128
SPAN = 128
MESH = pl.DeviceIdType.MESH
F32 = jnp.float32
BF16 = jnp.bfloat16


def dot(a, b, ca, cb):
    return lax.dot_general(a, b, (((ca,), (cb,)), ((), ())), preferred_element_type=F32)


def kernel(
    n, ndp, chain, doc, gain, q_hbm, k_hbm, v_hbm, y_hbm,
    gq_hbm, gk_hbm, gv_hbm, gg_out,
    q, k, v, y, kvb, kvr, intra, attn, da, stb, qdo, bkr, gkp, gvp, gq, gk, gv,
    tag, tagl, tagr, ssq, inn, gsum, ga, gb,
    in_sem, out_sem, ks, kr, bs, br, ts, tr, gas, gar, gbs, gbr,
):
    me = lax.axis_index("ctx")
    mydp = lax.axis_index("dp")
    right, left = lax.rem(me + 1, n), lax.rem(me + n - 1, n)
    has_right, has_left = me < n - 1, me > 0
    hps = HEADS // ndp

    loads = [
        pltpu.make_async_copy(src, dst, in_sem.at[i])
        for i, (src, dst) in enumerate(((k_hbm, k), (v_hbm, v), (q_hbm, q), (y_hbm, y)))
    ]
    for load in loads:
        load.start()

    barrier = pltpu.get_barrier_semaphore()
    for o in range(1, n):
        pl.semaphore_signal(barrier, inc=1, device_id={"ctx": lax.rem(me + o, n)}, device_id_type=MESH)
    for o in range(1, ndp):
        pl.semaphore_signal(barrier, inc=1, device_id={"dp": lax.rem(mydp + o, ndp)}, device_id_type=MESH)

    def cols(h):
        return pl.ds(pl.multiple_of(h * DIM, DIM), DIM)

    def remote(src, dst, s, r, where):
        return pltpu.make_async_remote_copy(
            src_ref=src, dst_ref=dst, send_sem=s, recv_sem=r, device_id=where, device_id_type=MESH
        )

    def kv_copy(h):
        return remote(kvb.at[h], kvr.at[h], ks.at[h], kr.at[h], {"ctx": right})

    def back_copy(h):
        return remote(qdo.at[h], bkr.at[h], bs.at[h], br.at[h], {"ctx": left})

    tag_right = remote(tag, tagl, ts.at[0], tr.at[0], {"ctx": right})
    tag_left = remote(tag, tagr, ts.at[1], tr.at[1], {"ctx": left})

    own = (doc[0, 0] + 1).astype(F32)
    tag[...] = jnp.full((8, 128), own, F32)

    @pl.when(jnp.logical_not(has_left))
    def _():
        tagl[...] = jnp.full((8, 128), -1.0, F32)
        kvr[...] = jnp.zeros_like(kvr)

    @pl.when(jnp.logical_not(has_right))
    def _():
        tagr[...] = jnp.full((8, 128), -1.0, F32)
        bkr[...] = jnp.zeros_like(bkr)

    loads[0].wait()
    loads[1].wait()
    pl.semaphore_wait(barrier, n - 1 + ndp - 1)

    @pl.when(has_right)
    def _():
        tag_right.start()

    @pl.when(has_left)
    def _():
        tag_left.start()

    def kv_step(h, _):
        kvb[h] = dot(k[:, cols(h)], v[:, cols(h)], 0, 0)
        if not chain:

            @pl.when(has_right)
            def _():
                kv_copy(h).start()

        return 0

    lax.fori_loop(0, HEADS, kv_step, 0, unroll=2)
    loads[2].wait()
    loads[3].wait()

    rows = lax.broadcasted_iota(jnp.int32, (SPAN, SPAN), 0)
    lanes = lax.broadcasted_iota(jnp.int32, (SPAN, SPAN), 1)
    causal = rows >= lanes

    def local_step(h, _):
        c = cols(h)
        w = jnp.where(causal, dot(q[:, c], k[:, c], 1, 1), 0.0).astype(BF16)
        intra[:, c] = w
        attn[:, c] = dot(w, v[:, c], 1, 0)
        return 0

    lax.fori_loop(0, HEADS, local_step, 0, unroll=2)

    @pl.when(has_left)
    def _():
        tag_right.wait_recv()

    @pl.when(has_right)
    def _():
        tag_left.wait_recv()

    from_left = jnp.broadcast_to(tagl[0:1, :] == tag[0:1, :], (DIM, DIM))
    from_right = jnp.broadcast_to(tagr[0:1, :] == tag[0:1, :], (DIM, DIM))

    ssq[...] = jnp.zeros_like(ssq)
    inn[...] = jnp.zeros_like(inn)

    def attn_step(h, _):
        c = cols(h)

        @pl.when(has_left)
        def _():
            kv_copy(h).wait_recv()

        state = jnp.where(from_left, kvr[h], 0.0)
        if chain:
            kvb[h] = kvb[h] + state

            @pl.when(has_right)
            def _():
                kv_copy(h).start()

        sb = state.astype(BF16)
        stb[h] = sb
        a = attn[:, c] + dot(q[:, c], sb, 1, 0)
        attn[:, c] = a
        ssq[...] += a * a
        inn[...] += y[:, c].astype(F32) * gain[:, c].astype(F32) * a
        return 0

    lax.fori_loop(0, HEADS, attn_step, 0, unroll=2)

    features = HEADS * DIM
    inv = 1.0 / jnp.sqrt(jnp.sum(ssq[...], axis=-1, keepdims=True) / features + 1e-05)
    coef = jnp.sum(inn[...], axis=-1, keepdims=True) * inv**3 / features
    inv_b = jnp.broadcast_to(inv, (SPAN, DIM))
    coef_b = jnp.broadcast_to(coef, (SPAN, DIM))

    def da_step(h, _):
        c = cols(h)
        a = attn[:, c]
        g = y[:, c].astype(F32)
        d = (g * gain[:, c].astype(F32) * inv_b - a * coef_b).astype(BF16)
        da[:, c] = d
        qdo[h] = dot(q[:, c], d, 0, 0)
        gsum[h] = jnp.sum(g * a * inv_b, axis=0, keepdims=True)
        if not chain:

            @pl.when(has_left)
            def _():
                back_copy(h).start()

        return 0

    lax.fori_loop(0, HEADS, da_step, 0, unroll=2)

    def ga_copy(o):
        to = lax.rem(mydp + o, ndp)
        return remote(
            gsum.at[pl.ds(to * hps, hps)], ga.at[o - 1], gas.at[o - 1], gar.at[o - 1], {"dp": to}
        )

    for o in range(1, ndp):
        ga_copy(o).start()

    def grad_step(h, _):
        c = cols(h)
        d = da[:, c]
        w = jnp.where(causal, dot(d, v[:, c], 1, 1), 0.0).astype(BF16)
        gq[:, c] = (dot(w, k[:, c], 1, 0) + dot(d, stb[h], 1, 1)).astype(BF16)
        gkp[:, c] = dot(w, q[:, c], 0, 0)
        gvp[:, c] = dot(intra[:, c], d, 0, 0)
        return 0

    lax.fori_loop(0, HEADS, grad_step, 0, unroll=2)
    out_q = pltpu.make_async_copy(gq, gq_hbm, out_sem.at[0])
    out_q.start()

    for o in range(1, ndp):
        ga_copy(o).wait_recv()
    mine = gsum[pl.ds(mydp * hps, hps)]
    for o in range(1, ndp):
        mine = mine + ga[o - 1]
    gb[me] = mine

    def gb_send(o):
        return remote(gb.at[me], gb.at[me], gbs.at[o - 1], gbr.at[o - 1], {"ctx": lax.rem(me + o, n)})

    def gb_recv(o):
        source = lax.rem(me + n - o, n)
        return remote(gb.at[source], gb.at[source], gbs.at[o - 1], gbr.at[o - 1], {"ctx": lax.rem(me + o, n)})

    for o in range(1, n):
        gb_send(o).start()

    def back_step(h, _):
        c = cols(h)

        @pl.when(has_right)
        def _():
            back_copy(h).wait_recv()

        back = jnp.where(from_right, bkr[h], 0.0)
        if chain:
            qdo[h] = qdo[h] + back

            @pl.when(has_left)
            def _():
                back_copy(h).start()

        bb = back.astype(BF16)
        gk[:, c] = (gkp[:, c] + dot(v[:, c], bb, 1, 1)).astype(BF16)
        gv[:, c] = (gvp[:, c] + dot(k[:, c], bb, 1, 0)).astype(BF16)
        return 0

    lax.fori_loop(0, HEADS, back_step, 0, unroll=2)
    out_k = pltpu.make_async_copy(gk, gk_hbm, out_sem.at[1])
    out_v = pltpu.make_async_copy(gv, gv_hbm, out_sem.at[2])
    out_k.start()
    out_v.start()

    for o in range(1, n):
        gb_recv(o).wait_recv()
    total = gb[0]
    for i in range(1, n):
        total = total + gb[i]
    gg_out[...] = total

    for o in range(1, n):
        gb_send(o).wait_send()
    for o in range(1, ndp):
        ga_copy(o).wait_send()

    @pl.when(has_right)
    def _():
        tag_right.wait_send()

        def done(h, _):
            kv_copy(h).wait_send()
            return 0

        lax.fori_loop(0, HEADS, done, 0)

    @pl.when(has_left)
    def _():
        tag_left.wait_send()

        def done(h, _):
            back_copy(h).wait_send()
            return 0

        lax.fori_loop(0, HEADS, done, 0)

    out_q.wait()
    out_k.wait()
    out_v.wait()


def per_device(n, ndp, queries, keys, values, grad_normed, gain, doc_ids):
    batch, length, features = queries.shape
    flat = (length, features)
    hps = HEADS // ndp
    chain = n // 2 > 2
    vmem = pltpu.VMEM
    dma = pltpu.SemaphoreType.DMA
    hbm = pl.BlockSpec(memory_space=pl.ANY)
    big = jax.ShapeDtypeStruct(flat, BF16)
    square = (HEADS, DIM, DIM)
    gq, gk, gv, gg = pl.pallas_call(
        functools.partial(kernel, n, ndp, chain),
        out_shape=(big, big, big, jax.ShapeDtypeStruct((hps, 1, DIM), F32)),
        in_specs=[
            pl.BlockSpec(memory_space=pltpu.SMEM),
            pl.BlockSpec(memory_space=pltpu.VMEM),
            hbm, hbm, hbm, hbm,
        ],
        out_specs=(hbm, hbm, hbm, pl.BlockSpec(memory_space=pltpu.VMEM)),
        scratch_shapes=[
            vmem(flat, BF16), vmem(flat, BF16), vmem(flat, BF16), vmem(flat, BF16),
            vmem(square, F32), vmem(square, F32),
            vmem(flat, BF16), vmem(flat, F32), vmem(flat, BF16), vmem(square, BF16),
            vmem(square, F32), vmem(square, F32),
            vmem(flat, F32), vmem(flat, F32),
            vmem(flat, BF16), vmem(flat, BF16), vmem(flat, BF16),
            vmem((8, DIM), F32), vmem((8, DIM), F32), vmem((8, DIM), F32),
            vmem((SPAN, DIM), F32), vmem((SPAN, DIM), F32),
            vmem((HEADS, 1, DIM), F32), vmem((ndp - 1, hps, 1, DIM), F32), vmem((n, hps, 1, DIM), F32),
            dma((4,)), dma((3,)),
            dma((HEADS,)), dma((HEADS,)), dma((HEADS,)), dma((HEADS,)),
            dma((2,)), dma((2,)),
            dma((ndp - 1,)), dma((ndp - 1,)), dma((n - 1,)), dma((n - 1,)),
        ],
        compiler_params=pltpu.CompilerParams(
            collective_id=0, has_side_effects=True, vmem_limit_bytes=40 << 20
        ),
        name="lin_attn_bwd",
    )(
        doc_ids,
        gain.reshape(1, features),
        queries.reshape(flat),
        keys.reshape(flat),
        values.reshape(flat),
        grad_normed.reshape(flat),
    )
    whole = (batch, length, features)
    return gq.reshape(whole), gk.reshape(whole), gv.reshape(whole), gg.reshape(features // ndp)


def solution(mesh):
    rows = P(("group", "dp"), "ctx", None)
    return jax.shard_map(
        functools.partial(per_device, mesh.shape["ctx"], mesh.shape["dp"]),
        mesh=mesh,
        in_specs=(rows, rows, rows, rows, P(), P(("group", "dp"), "ctx")),
        out_specs=(rows, rows, rows, P(("group", "dp"))),
        check_vma=False,
    )
```

```python
import functools

import jax
import jax.numpy as jnp
from jax import lax
from jax.experimental import pallas as pl
from jax.experimental.pallas import tpu as pltpu
from jax.sharding import PartitionSpec as P

HEADS = 16
DIM = 128
SPAN = 128
SHIFT = 4
MESH = pl.DeviceIdType.MESH
F32 = jnp.float32
BF16 = jnp.bfloat16


def dot(a, b, ca, cb):
    return lax.dot_general(a, b, (((ca,), (cb,)), ((), ())), preferred_element_type=F32)


def kernel(
    n, ndp, chain, shift, doc, gain_hbm, q_hbm, k_hbm, v_hbm, y_hbm,
    gq, gk, gv, gg_out,
    gain, q, k, v, y, kvb, kvr, intra, attn, da, stb, qdo, bkr, gkp, gvp,
    tag, tagl, tagr, ssq, inn, gsum, ga, gb, stage, rstage, dsq, dnn, stat, statr, scal, scalr,
    in_sem, ks, kr, bs, br, ts, tr, gas, gar, gbs, gbr, ss, sr, ms, mr,
):
    me = lax.axis_index("ctx")
    mydp = lax.axis_index("dp")
    right, left = lax.rem(me + 1, n), lax.rem(me + n - 1, n)
    has_right, has_left = me < n - 1, me > 0
    hps = HEADS // ndp
    plain = HEADS - shift
    features = HEADS * DIM

    loads = [
        pltpu.make_async_copy(src, dst, in_sem.at[i])
        for i, (src, dst) in enumerate(
            ((k_hbm, k), (v_hbm, v), (q_hbm, q), (y_hbm, y), (gain_hbm, gain))
        )
    ]
    for load in loads:
        load.start()

    barrier = pltpu.get_barrier_semaphore()
    for o in range(1, n):
        pl.semaphore_signal(barrier, inc=1, device_id={"ctx": lax.rem(me + o, n)}, device_id_type=MESH)
    for o in range(1, ndp):
        pl.semaphore_signal(barrier, inc=1, device_id={"dp": lax.rem(mydp + o, ndp)}, device_id_type=MESH)

    def cols(h):
        return pl.ds(pl.multiple_of(h * DIM, DIM), DIM)

    def loop(first, last, body, unroll=2):
        def step(h, _):
            body(h)
            return 0

        if last > first:
            lax.fori_loop(first, last, step, 0, unroll=unroll if (last - first) % unroll == 0 else 1)

    def remote(src, dst, s, r, where):
        return pltpu.make_async_remote_copy(
            src_ref=src, dst_ref=dst, send_sem=s, recv_sem=r, device_id=where, device_id_type=MESH
        )

    to_right, to_left = {"ctx": right}, {"ctx": left}

    def kv_copy(h):
        return remote(kvb.at[h], kvr.at[h], ks.at[h], kr.at[h], to_right)

    def back_copy(h):
        return remote(qdo.at[h], bkr.at[h], bs.at[h], br.at[h], to_left)

    def stage_copy(j):
        return remote(stage.at[j], rstage.at[j], ss.at[j], sr.at[j], to_left)

    tag_right = remote(tag, tagl, ts.at[0], tr.at[0], to_right)
    tag_left = remote(tag, tagr, ts.at[1], tr.at[1], to_left)
    stat_right = remote(stat, statr, ms.at[0], mr.at[0], to_right)
    scal_left = remote(scal, scalr, ms.at[1], mr.at[1], to_left)

    own = (doc[0, 0] + 1).astype(F32)
    tag[...] = jnp.full((8, 128), own, F32)
    ssq[...] = jnp.zeros_like(ssq)
    inn[...] = jnp.zeros_like(inn)
    dsq[...] = jnp.zeros_like(dsq)
    dnn[...] = jnp.zeros_like(dnn)

    @pl.when(jnp.logical_not(has_left))
    def _():
        tagl[...] = jnp.full((8, 128), -1.0, F32)
        kvr[...] = jnp.zeros_like(kvr)
        statr[...] = jnp.zeros_like(statr)

    @pl.when(jnp.logical_not(has_right))
    def _():
        tagr[...] = jnp.full((8, 128), -1.0, F32)
        bkr[...] = jnp.zeros_like(bkr)

    rows = lax.broadcasted_iota(jnp.int32, (SPAN, SPAN), 0)
    lanes = lax.broadcasted_iota(jnp.int32, (SPAN, SPAN), 1)
    causal = rows >= lanes

    loads[0].wait()
    loads[1].wait()
    pl.semaphore_wait(barrier, n - 1 + ndp - 1)

    @pl.when(has_right)
    def _():
        tag_right.start()

    @pl.when(has_left)
    def _():
        tag_left.start()

    def kv_only(h):
        kvb[h] = dot(k[:, cols(h)], v[:, cols(h)], 0, 0)

    def kv_step(h):
        kv_only(h)
        if not chain:

            @pl.when(has_right)
            def _():
                kv_copy(h).start()

    def local_step(h):
        c = cols(h)
        w = jnp.where(causal, dot(q[:, c], k[:, c], 1, 1), 0.0).astype(BF16)
        intra[:, c] = w
        attn[:, c] = dot(w, v[:, c], 1, 0)

    def stage_step(j):
        h = plain + j
        c = cols(h)
        local_step(h)
        a = attn[:, c]
        g = y[:, c].astype(F32)
        stage[j, 0] = q[:, c].astype(F32)
        stage[j, 1] = g
        stage[j, 2] = a

        @pl.when(has_left)
        def _():
            stage_copy(j).start()

        ssq[...] += a * a
        inn[...] += g * gain[:, c].astype(F32) * a

    ahead = 4
    loop(0, ahead, kv_step)
    for load in loads[2:]:
        load.wait()
    loop(0, shift, stage_step)
    loop(ahead, plain, kv_step)
    loop(plain, HEADS, kv_only)
    loop(0, plain, local_step)

    @pl.when(has_left)
    def _():
        tag_right.wait_recv()

    @pl.when(has_right)
    def _():
        tag_left.wait_recv()

    from_left = jnp.broadcast_to(tagl[0:1, :] == tag[0:1, :], (DIM, DIM))
    from_right = jnp.broadcast_to(tagr[0:1, :] == tag[0:1, :], (DIM, DIM))

    def state_step(h):
        c = cols(h)

        @pl.when(has_left)
        def _():
            kv_copy(h).wait_recv()

        state = jnp.where(from_left, kvr[h], 0.0)
        if chain:
            kvb[h] = kvb[h] + state

            @pl.when(has_right)
            def _():
                kv_copy(h).start()

        sb = state.astype(BF16)
        stb[h] = sb
        a = attn[:, c] + dot(q[:, c], sb, 1, 0)
        attn[:, c] = a
        return a

    def attn_step(h):
        c = cols(h)
        a = state_step(h)
        ssq[...] += a * a
        inn[...] += y[:, c].astype(F32) * gain[:, c].astype(F32) * a

    def helper_step(j):
        c = cols(plain + j)
        stage_copy(j).wait_recv()
        kb = jnp.where(from_right, kvb[plain + j], 0.0).astype(BF16)
        x = dot(rstage[j, 0].astype(BF16), kb, 1, 0)
        a = rstage[j, 2]
        dsq[...] += (2.0 * a + x) * x
        dnn[...] += rstage[j, 1] * gain[:, c].astype(F32) * x
        rstage[j, 2] = a + x

    if shift:
        for j in range(shift):
            loop(plain * j // shift, plain * (j + 1) // shift, attn_step, 3)

            @pl.when(has_right)
            def _():
                helper_step(j)

        @pl.when(has_right)
        def _():
            stat[0] = jnp.sum(jnp.transpose(dsq[...]).reshape(16, 8, SPAN), axis=0)
            stat[1] = jnp.sum(jnp.transpose(dnn[...]).reshape(16, 8, SPAN), axis=0)
            stat_right.start()

            def send(j):
                kv_copy(plain + j).start()

            loop(0, shift, send)

        @pl.when(has_left)
        def _():
            stat_right.wait_recv()

        extra_sq = jnp.transpose(jnp.broadcast_to(jnp.sum(statr[0], axis=0, keepdims=True), (DIM, SPAN)))
        extra_in = jnp.transpose(jnp.broadcast_to(jnp.sum(statr[1], axis=0, keepdims=True), (DIM, SPAN)))
    else:
        loop(0, HEADS, attn_step)
        extra_sq = extra_in = 0.0

    mean = jnp.broadcast_to(jnp.sum(ssq[...], axis=-1, keepdims=True), (SPAN, DIM)) + extra_sq
    inner = jnp.broadcast_to(jnp.sum(inn[...], axis=-1, keepdims=True), (SPAN, DIM)) + extra_in
    inv = 1.0 / jnp.sqrt(mean / features + 1e-05)
    coef = inner * inv**3 / features

    if shift:
        scal[0] = jnp.transpose(inv)[0:8]
        scal[1] = jnp.transpose(coef)[0:8]

        @pl.when(has_left)
        def _():
            scal_left.start()

    def da_step(h):
        c = cols(h)
        a = attn[:, c]
        g = y[:, c].astype(F32)
        d = (g * gain[:, c].astype(F32) * inv - a * coef).astype(BF16)
        da[:, c] = d
        gsum[h] = jnp.sum(g * a * inv, axis=0, keepdims=True)
        return d

    def send_step(h):
        qdo[h] = dot(q[:, cols(h)], da_step(h), 0, 0)
        if not chain:

            @pl.when(has_left)
            def _():
                back_copy(h).start()

    def grad_step(h):
        c = cols(h)
        d = da[:, c]
        w = jnp.where(causal, dot(d, v[:, c], 1, 1), 0.0).astype(BF16)
        gq[:, c] = (dot(w, k[:, c], 1, 0) + dot(d, stb[h], 1, 1)).astype(BF16)
        gkp[:, c] = dot(w, q[:, c], 0, 0)
        gvp[:, c] = dot(intra[:, c], d, 0, 0)

    loop(0, plain, send_step)

    def late_step(h):
        state_step(h)
        da_step(h)

    if shift:
        loop(0, plain, grad_step)
        loop(plain, HEADS, late_step)

    def ga_copy(o):
        to = lax.rem(mydp + o, ndp)
        return remote(
            gsum.at[pl.ds(to * hps, hps)], ga.at[o - 1], gas.at[o - 1], gar.at[o - 1], {"dp": to}
        )

    for o in range(1, ndp):
        ga_copy(o).start()

    loop(plain if shift else 0, HEADS, grad_step)

    def finish(h, back):
        c = cols(h)
        bb = back.astype(BF16)
        gk[:, c] = (gkp[:, c] + dot(v[:, c], bb, 1, 1)).astype(BF16)
        gv[:, c] = (gvp[:, c] + dot(k[:, c], bb, 1, 0)).astype(BF16)

    if shift:

        @pl.when(has_right)
        def _():
            scal_left.wait_recv()
            r_inv = jnp.transpose(jnp.broadcast_to(scalr[0, 0:1], (DIM, SPAN)))
            r_coef = jnp.transpose(jnp.broadcast_to(scalr[1, 0:1], (DIM, SPAN)))

            def near(j):
                c = cols(plain + j)
                d = (rstage[j, 1] * gain[:, c].astype(F32) * r_inv - rstage[j, 2] * r_coef).astype(BF16)
                bkr[plain + j] = dot(rstage[j, 0].astype(BF16), d, 0, 0)

            loop(0, shift, near)

        def near_finish(h):
            finish(h, jnp.where(from_right, bkr[h], 0.0))

        loop(plain, HEADS, near_finish)

    for o in range(1, ndp):
        ga_copy(o).wait_recv()
    mine = gsum[pl.ds(mydp * hps, hps)]
    for o in range(1, ndp):
        mine = mine + ga[o - 1]
    gb[me] = mine

    def gb_send(o):
        return remote(gb.at[me], gb.at[me], gbs.at[o - 1], gbr.at[o - 1], {"ctx": lax.rem(me + o, n)})

    def gb_recv(o):
        source = lax.rem(me + n - o, n)
        return remote(gb.at[source], gb.at[source], gbs.at[o - 1], gbr.at[o - 1], {"ctx": lax.rem(me + o, n)})

    for o in range(1, n):
        gb_send(o).start()

    def back_step(h):
        @pl.when(has_right)
        def _():
            back_copy(h).wait_recv()

        back = jnp.where(from_right, bkr[h], 0.0)
        if chain:
            qdo[h] = qdo[h] + back

            @pl.when(has_left)
            def _():
                back_copy(h).start()

        finish(h, back)

    loop(0, plain, back_step)

    for o in range(1, n):
        gb_recv(o).wait_recv()
    total = gb[0]
    for i in range(1, n):
        total = total + gb[i]
    gg_out[...] = total

    for o in range(1, n):
        gb_send(o).wait_send()
    for o in range(1, ndp):
        ga_copy(o).wait_send()

    @pl.when(has_right)
    def _():
        tag_right.wait_send()
        loop(0, HEADS, lambda h: kv_copy(h).wait_send(), 1)
        if shift:
            stat_right.wait_send()

    @pl.when(has_left)
    def _():
        tag_left.wait_send()
        loop(0, plain, lambda h: back_copy(h).wait_send(), 1)
        if shift:
            loop(0, shift, lambda j: stage_copy(j).wait_send(), 1)
            scal_left.wait_send()


def per_device(n, ndp, queries, keys, values, grad_normed, gain, doc_ids):
    batch, length, features = queries.shape
    flat = (length, features)
    hps = HEADS // ndp
    chain = n // 2 > 2
    shift = 0 if chain else SHIFT
    spare = max(shift, 1)
    vmem = pltpu.VMEM
    dma = pltpu.SemaphoreType.DMA
    hbm = pl.BlockSpec(memory_space=pltpu.HBM)
    near = pl.BlockSpec(memory_space=pltpu.VMEM)
    big = jax.ShapeDtypeStruct(flat, BF16)
    square = (HEADS, DIM, DIM)
    small = (2, 8, DIM)
    gq, gk, gv, gg = pl.pallas_call(
        functools.partial(kernel, n, ndp, chain, shift),
        out_shape=(big, big, big, jax.ShapeDtypeStruct((hps, 1, DIM), F32)),
        in_specs=[pl.BlockSpec(memory_space=pltpu.SMEM), hbm, hbm, hbm, hbm, hbm],
        out_specs=(near, near, near, near),
        scratch_shapes=[
            vmem((1, features), BF16),
            vmem(flat, BF16), vmem(flat, BF16), vmem(flat, BF16), vmem(flat, BF16),
            vmem(square, F32), vmem(square, F32),
            vmem(flat, BF16), vmem(flat, F32), vmem(flat, BF16), vmem(square, BF16),
            vmem(square, F32), vmem(square, F32),
            vmem(flat, F32), vmem(flat, F32),
            vmem((8, DIM), F32), vmem((8, DIM), F32), vmem((8, DIM), F32),
            vmem((SPAN, DIM), F32), vmem((SPAN, DIM), F32),
            vmem((HEADS, 1, DIM), F32), vmem((ndp - 1, hps, 1, DIM), F32), vmem((n, hps, 1, DIM), F32),
            vmem((spare, 3, SPAN, DIM), F32), vmem((spare, 3, SPAN, DIM), F32),
            vmem((SPAN, DIM), F32), vmem((SPAN, DIM), F32),
            vmem(small, F32), vmem(small, F32), vmem(small, F32), vmem(small, F32),
            dma((5,)),
            dma((HEADS,)), dma((HEADS,)), dma((HEADS,)), dma((HEADS,)),
            dma((2,)), dma((2,)),
            dma((ndp - 1,)), dma((ndp - 1,)), dma((n - 1,)), dma((n - 1,)),
            dma((spare,)), dma((spare,)), dma((2,)), dma((2,)),
        ],
        compiler_params=pltpu.CompilerParams(
            collective_id=0, has_side_effects=True, vmem_limit_bytes=62 << 20
        ),
        name="lin_attn_bwd",
    )(
        doc_ids,
        gain.reshape(1, features),
        queries.reshape(flat),
        keys.reshape(flat),
        values.reshape(flat),
        grad_normed.reshape(flat),
    )
    whole = (batch, length, features)
    return gq.reshape(whole), gk.reshape(whole), gv.reshape(whole), gg.reshape(features // ndp)


def solution(mesh):
    rows = P(("group", "dp"), "ctx", None)
    return jax.shard_map(
        functools.partial(per_device, mesh.shape["ctx"], mesh.shape["dp"]),
        mesh=mesh,
        in_specs=(rows, rows, rows, rows, P(), P(("group", "dp"), "ctx")),
        out_specs=(rows, rows, rows, P(("group", "dp"))),
        check_vma=False,
    )
```

```python
import functools

import jax
import jax.numpy as jnp
from jax import lax
from jax.experimental import pallas as pl
from jax.experimental.pallas import tpu as pltpu
from jax.sharding import PartitionSpec as P

HEADS = 16
DIM = 128
SPAN = 128
SHIFT = 4
GROUP = 4
STAGE = 2
MESH = pl.DeviceIdType.MESH
F32 = jnp.float32
BF16 = jnp.bfloat16


def dot(a, b, ca, cb):
    return lax.dot_general(a, b, (((ca,), (cb,)), ((), ())), preferred_element_type=F32)


def kernel(
    n, ndp, chain, shift, doc, gain_hbm, q_hbm, k_hbm, v_hbm, y_hbm,
    gq, gk, gv, gg_out,
    gain_in, gain, q, k, v, y, kvb, kvr, intra, attn, da, stb, qdo, bkr, gkp, gvp,
    tag, tagl, tagr, ssq, inn, gsum, ga, gb, stage, rstage, dsq, dnn, stat, statr, scal, scalr,
    in_sem, ks, kr, bs, br, ts, tr, gas, gar, gbs, gbr, ss, sr, ms, mr,
):
    me = lax.axis_index("ctx")
    mydp = lax.axis_index("dp")
    right, left = lax.rem(me + 1, n), lax.rem(me + n - 1, n)
    has_right, has_left = me < n - 1, me > 0
    hps = HEADS // ndp
    plain = HEADS - shift
    features = HEADS * DIM

    loads = [
        pltpu.make_async_copy(src, dst, in_sem.at[i])
        for i, (src, dst) in enumerate(
            ((k_hbm, k), (v_hbm, v), (q_hbm, q), (y_hbm, y), (gain_hbm, gain_in))
        )
    ]
    for load in loads:
        load.start()

    barrier = pltpu.get_barrier_semaphore()
    for o in range(1, n):
        pl.semaphore_signal(barrier, inc=1, device_id={"ctx": lax.rem(me + o, n)}, device_id_type=MESH)
    for o in range(1, ndp):
        pl.semaphore_signal(barrier, inc=1, device_id={"dp": lax.rem(mydp + o, ndp)}, device_id_type=MESH)

    def cols(h):
        return pl.ds(pl.multiple_of(h * DIM, DIM), DIM)

    def loop(first, last, body, group=GROUP):
        whole = (last - first) // group

        def step(g, _):
            body([first + g * group + i for i in range(group)])
            return 0

        if whole == 1:
            step(0, 0)
        elif whole > 1:
            lax.fori_loop(0, whole, step, 0)
        if first + whole * group < last:
            body(list(range(first + whole * group, last)))

    def each(first, last, body):
        def step(h, _):
            body(h)
            return 0

        if last > first:
            lax.fori_loop(first, last, step, 0)

    def remote(src, dst, s, r, where):
        return pltpu.make_async_remote_copy(
            src_ref=src, dst_ref=dst, send_sem=s, recv_sem=r, device_id=where, device_id_type=MESH
        )

    to_right, to_left = {"ctx": right}, {"ctx": left}

    def kv_copy(h):
        return remote(kvb.at[h], kvr.at[h], ks.at[h], kr.at[h], to_right)

    def back_copy(h):
        return remote(qdo.at[h], bkr.at[h], bs.at[h], br.at[h], to_left)

    def stage_copy(j):
        return remote(stage.at[j], rstage.at[j], ss.at[j], sr.at[j], to_left)

    tag_right = remote(tag, tagl, ts.at[0], tr.at[0], to_right)
    tag_left = remote(tag, tagr, ts.at[1], tr.at[1], to_left)
    stat_right = remote(stat, statr, ms.at[0], mr.at[0], to_right)
    scal_left = remote(scal, scalr, ms.at[1], mr.at[1], to_left)

    own = (doc[0, 0] + 1).astype(F32)
    tag[...] = jnp.full((8, 128), own, F32)
    ssq[...] = jnp.zeros_like(ssq)
    inn[...] = jnp.zeros_like(inn)
    dsq[...] = jnp.zeros_like(dsq)
    dnn[...] = jnp.zeros_like(dnn)

    @pl.when(jnp.logical_not(has_left))
    def _():
        tagl[...] = jnp.full((8, 128), -1.0, F32)
        kvr[...] = jnp.zeros_like(kvr)
        statr[...] = jnp.zeros_like(statr)

    @pl.when(jnp.logical_not(has_right))
    def _():
        tagr[...] = jnp.full((8, 128), -1.0, F32)
        bkr[...] = jnp.zeros_like(bkr)

    rows = lax.broadcasted_iota(jnp.int32, (SPAN, SPAN), 0)
    lanes = lax.broadcasted_iota(jnp.int32, (SPAN, SPAN), 1)
    causal = rows >= lanes

    loads[0].wait()
    loads[1].wait()
    pl.semaphore_wait(barrier, n - 1 + ndp - 1)

    @pl.when(has_right)
    def _():
        tag_right.start()

    @pl.when(has_left)
    def _():
        tag_left.start()

    def kv_only(hs):
        for h, m in [(h, dot(k[:, cols(h)], v[:, cols(h)], 0, 0)) for h in hs]:
            kvb[h] = m

    def kv_step(hs):
        kv_only(hs)
        if not chain:

            @pl.when(has_right)
            def _():
                for h in hs:
                    kv_copy(h).start()

    def local_step(hs):
        scores = [dot(q[:, cols(h)], k[:, cols(h)], 1, 1) for h in hs]
        ws = [jnp.where(causal, x, 0.0).astype(BF16) for x in scores]
        outs = [dot(w, v[:, cols(h)], 1, 0) for h, w in zip(hs, ws)]
        for h, w, a in zip(hs, ws, outs):
            intra[:, cols(h)] = w
            attn[:, cols(h)] = a
        return outs

    def sums(terms):
        total = terms[0]
        for term in terms[1:]:
            total = total + term
        return total

    def norm_sums(hs, outs):
        ssq[...] += sums([a * a for a in outs])
        inn[...] += sums([y[:, cols(h)].astype(F32) * gain[h] * a for h, a in zip(hs, outs)])

    def stage_step(js):
        hs = [plain + j for j in js]
        outs = local_step(hs)
        for j, h, a in zip(js, hs, outs):
            stage[j, 0] = q[:, cols(h)].astype(F32)
            stage[j, 1] = y[:, cols(h)].astype(F32)
            stage[j, 2] = a

        @pl.when(has_left)
        def _():
            for j in js:
                stage_copy(j).start()

        norm_sums(hs, outs)

    ahead = min(GROUP, plain)
    loop(0, ahead, kv_step)
    for load in loads[2:]:
        load.wait()
    for h in range(HEADS):
        gain[h] = gain_in[h * DIM : (h + 1) * DIM].astype(F32).reshape(1, DIM)
    loop(0, shift, stage_step, STAGE)
    loop(ahead, plain, kv_step)
    loop(plain, HEADS, kv_only)
    loop(0, plain, local_step)

    @pl.when(has_left)
    def _():
        tag_right.wait_recv()

    @pl.when(has_right)
    def _():
        tag_left.wait_recv()

    from_left = jnp.broadcast_to(tagl[0:1, :] == tag[0:1, :], (DIM, DIM))
    from_right = jnp.broadcast_to(tagr[0:1, :] == tag[0:1, :], (DIM, DIM))

    def state_step(hs):
        @pl.when(has_left)
        def _():
            for h in hs:
                kv_copy(h).wait_recv()

        states = [jnp.where(from_left, kvr[h], 0.0) for h in hs]
        if chain:
            for h, state in zip(hs, states):
                kvb[h] = kvb[h] + state

            @pl.when(has_right)
            def _():
                for h in hs:
                    kv_copy(h).start()

        rounded = [state.astype(BF16) for state in states]
        outs = [attn[:, cols(h)] + dot(q[:, cols(h)], sb, 1, 0) for h, sb in zip(hs, rounded)]
        for h, sb, a in zip(hs, rounded, outs):
            stb[h] = sb
            attn[:, cols(h)] = a
        return outs

    def attn_step(hs):
        norm_sums(hs, state_step(hs))

    def helper_step(js):
        for j in js:
            stage_copy(j).wait_recv()
        kbs = [jnp.where(from_right, kvb[plain + j], 0.0).astype(BF16) for j in js]
        xs = [dot(rstage[j, 0].astype(BF16), kb, 1, 0) for j, kb in zip(js, kbs)]
        olds = [rstage[j, 2] for j in js]
        dsq[...] += sums([(2.0 * a + x) * x for a, x in zip(olds, xs)])
        dnn[...] += sums([rstage[j, 1] * gain[plain + j] * x for j, x in zip(js, xs)])
        for j, a, x in zip(js, olds, xs):
            rstage[j, 2] = a + x

    if shift:
        parts = max(shift // 2, 1)
        for p in range(parts):
            loop(plain * p // parts, plain * (p + 1) // parts, attn_step, 3)

            @pl.when(has_right)
            def _():
                helper_step(list(range(shift * p // parts, shift * (p + 1) // parts)))

        @pl.when(has_right)
        def _():
            stat[0] = jnp.sum(jnp.transpose(dsq[...]).reshape(16, 8, SPAN), axis=0)
            stat[1] = jnp.sum(jnp.transpose(dnn[...]).reshape(16, 8, SPAN), axis=0)
            stat_right.start()

            for j in range(shift):
                kv_copy(plain + j).start()

        @pl.when(has_left)
        def _():
            stat_right.wait_recv()

        extra_sq = jnp.transpose(jnp.broadcast_to(jnp.sum(statr[0], axis=0, keepdims=True), (DIM, SPAN)))
        extra_in = jnp.transpose(jnp.broadcast_to(jnp.sum(statr[1], axis=0, keepdims=True), (DIM, SPAN)))
    else:
        loop(0, HEADS, attn_step)
        extra_sq = extra_in = 0.0

    mean = jnp.broadcast_to(jnp.sum(ssq[...], axis=-1, keepdims=True), (SPAN, DIM)) + extra_sq
    inner = jnp.broadcast_to(jnp.sum(inn[...], axis=-1, keepdims=True), (SPAN, DIM)) + extra_in
    inv = 1.0 / jnp.sqrt(mean / features + 1e-05)
    coef = inner * inv**3 / features

    if shift:
        scal[0] = jnp.transpose(inv)[0:8]
        scal[1] = jnp.transpose(coef)[0:8]

        @pl.when(has_left)
        def _():
            scal_left.start()

    def da_step(hs):
        ds = []
        for h in hs:
            a = attn[:, cols(h)]
            g = y[:, cols(h)].astype(F32)
            ds.append((g * gain[h] * inv - a * coef).astype(BF16))
        for h, d in zip(hs, ds):
            da[:, cols(h)] = d
        return ds

    def gain_step(hs):
        rows_of = [
            jnp.sum(y[:, cols(h)].astype(F32) * attn[:, cols(h)] * inv, axis=0, keepdims=True) for h in hs
        ]
        for h, row in zip(hs, rows_of):
            gsum[h] = row

    def send_step(hs):
        for h, m in [(h, dot(q[:, cols(h)], d, 0, 0)) for h, d in zip(hs, da_step(hs))]:
            qdo[h] = m
        if not chain:

            @pl.when(has_left)
            def _():
                for h in hs:
                    back_copy(h).start()

    def grad_step(hs):
        ds = [da[:, cols(h)] for h in hs]
        scores = [dot(d, v[:, cols(h)], 1, 1) for h, d in zip(hs, ds)]
        ws = [jnp.where(causal, x, 0.0).astype(BF16) for x in scores]
        far = [dot(d, stb[h], 1, 1) for h, d in zip(hs, ds)]
        vs = [dot(intra[:, cols(h)], d, 0, 0) for h, d in zip(hs, ds)]
        qs = [dot(w, k[:, cols(h)], 1, 0) + f for h, w, f in zip(hs, ws, far)]
        kk = [dot(w, q[:, cols(h)], 0, 0) for h, w in zip(hs, ws)]
        for h, a, b, c in zip(hs, qs, kk, vs):
            gq[:, cols(h)] = a.astype(BF16)
            gkp[:, cols(h)] = b
            gvp[:, cols(h)] = c
        gain_step(hs)

    loop(0, plain, send_step)

    def late_step(hs):
        state_step(hs)
        da_step(hs)

    if shift:
        loop(0, plain, grad_step)
        loop(plain, HEADS, late_step)

    def ga_copy(o):
        to = lax.rem(mydp + o, ndp)
        return remote(
            gsum.at[pl.ds(to * hps, hps)], ga.at[o - 1], gas.at[o - 1], gar.at[o - 1], {"dp": to}
        )

    loop(plain if shift else 0, HEADS, grad_step)
    for o in range(1, ndp):
        ga_copy(o).start()

    def finish(hs, backs):
        rounded = [back.astype(BF16) for back in backs]
        kk = [gkp[:, cols(h)] + dot(v[:, cols(h)], bb, 1, 1) for h, bb in zip(hs, rounded)]
        vs = [gvp[:, cols(h)] + dot(k[:, cols(h)], bb, 1, 0) for h, bb in zip(hs, rounded)]
        for h, a, b in zip(hs, kk, vs):
            gk[:, cols(h)] = a.astype(BF16)
            gv[:, cols(h)] = b.astype(BF16)

    if shift:

        @pl.when(has_right)
        def _():
            scal_left.wait_recv()
            r_inv = jnp.transpose(jnp.broadcast_to(scalr[0, 0:1], (DIM, SPAN)))
            r_coef = jnp.transpose(jnp.broadcast_to(scalr[1, 0:1], (DIM, SPAN)))

            def near(js):
                ds = [
                    (rstage[j, 1] * gain[plain + j] * r_inv - rstage[j, 2] * r_coef).astype(BF16) for j in js
                ]
                for j, m in [(j, dot(rstage[j, 0].astype(BF16), d, 0, 0)) for j, d in zip(js, ds)]:
                    bkr[plain + j] = m

            loop(0, shift, near)

        def near_finish(hs):
            finish(hs, [jnp.where(from_right, bkr[h], 0.0) for h in hs])

        loop(plain, HEADS, near_finish)

    for o in range(1, ndp):
        ga_copy(o).wait_recv()
    mine = gsum[pl.ds(mydp * hps, hps)]
    for o in range(1, ndp):
        mine = mine + ga[o - 1]
    gb[me] = mine

    def gb_send(o):
        return remote(gb.at[me], gb.at[me], gbs.at[o - 1], gbr.at[o - 1], {"ctx": lax.rem(me + o, n)})

    def gb_recv(o):
        source = lax.rem(me + n - o, n)
        return remote(gb.at[source], gb.at[source], gbs.at[o - 1], gbr.at[o - 1], {"ctx": lax.rem(me + o, n)})

    for o in range(1, n):
        gb_send(o).start()

    def back_step(hs):
        @pl.when(has_right)
        def _():
            for h in hs:
                back_copy(h).wait_recv()

        backs = [jnp.where(from_right, bkr[h], 0.0) for h in hs]
        if chain:
            for h, back in zip(hs, backs):
                qdo[h] = qdo[h] + back

            @pl.when(has_left)
            def _():
                for h in hs:
                    back_copy(h).start()

        finish(hs, backs)

    loop(0, plain, back_step)

    for o in range(1, n):
        gb_recv(o).wait_recv()
    total = gb[0]
    for i in range(1, n):
        total = total + gb[i]
    gg_out[...] = total

    for o in range(1, n):
        gb_send(o).wait_send()
    for o in range(1, ndp):
        ga_copy(o).wait_send()

    @pl.when(has_right)
    def _():
        tag_right.wait_send()
        each(0, HEADS, lambda h: kv_copy(h).wait_send())
        if shift:
            stat_right.wait_send()

    @pl.when(has_left)
    def _():
        tag_left.wait_send()
        each(0, plain, lambda h: back_copy(h).wait_send())
        if shift:
            each(0, shift, lambda j: stage_copy(j).wait_send())
            scal_left.wait_send()


def writer(*refs):
    ins, outs, sem = refs[:4], refs[4:8], refs[8]
    copies = [pltpu.make_async_copy(a, b, sem.at[i]) for i, (a, b) in enumerate(zip(ins, outs))]
    for copy in copies:
        copy.start()
    for copy in copies:
        copy.wait()


def per_device(n, ndp, queries, keys, values, grad_normed, gain, doc_ids):
    batch, length, features = queries.shape
    flat = (length, features)
    hps = HEADS // ndp
    chain = n // 2 > 2
    shift = 0 if chain else SHIFT
    spare = max(shift, 1)
    vmem = pltpu.VMEM
    dma = pltpu.SemaphoreType.DMA
    hbm = pl.BlockSpec(memory_space=pltpu.HBM)
    near = pl.BlockSpec(memory_space=pltpu.VMEM)
    big = jax.ShapeDtypeStruct(flat, BF16)
    square = (HEADS, DIM, DIM)
    small = (2, 8, DIM)
    gq, gk, gv, gg = pl.pallas_call(
        functools.partial(kernel, n, ndp, chain, shift),
        out_shape=(big, big, big, jax.ShapeDtypeStruct((hps, 1, DIM), F32)),
        in_specs=[pl.BlockSpec(memory_space=pltpu.SMEM), hbm, hbm, hbm, hbm, hbm],
        out_specs=(near, near, near, near),
        scratch_shapes=[
            vmem((features,), BF16), vmem((HEADS, 1, DIM), F32),
            vmem(flat, BF16), vmem(flat, BF16), vmem(flat, BF16), vmem(flat, BF16),
            vmem(square, F32), vmem(square, F32),
            vmem(flat, BF16), vmem(flat, F32), vmem(flat, BF16), vmem(square, BF16),
            vmem(square, F32), vmem(square, F32),
            vmem(flat, F32), vmem(flat, F32),
            vmem((8, DIM), F32), vmem((8, DIM), F32), vmem((8, DIM), F32),
            vmem((SPAN, DIM), F32), vmem((SPAN, DIM), F32),
            vmem((HEADS, 1, DIM), F32), vmem((ndp - 1, hps, 1, DIM), F32), vmem((n, hps, 1, DIM), F32),
            vmem((spare, 3, SPAN, DIM), F32), vmem((spare, 3, SPAN, DIM), F32),
            vmem((SPAN, DIM), F32), vmem((SPAN, DIM), F32),
            vmem(small, F32), vmem(small, F32), vmem(small, F32), vmem(small, F32),
            dma((5,)),
            dma((HEADS,)), dma((HEADS,)), dma((HEADS,)), dma((HEADS,)),
            dma((2,)), dma((2,)),
            dma((ndp - 1,)), dma((ndp - 1,)), dma((n - 1,)), dma((n - 1,)),
            dma((spare,)), dma((spare,)), dma((2,)), dma((2,)),
        ],
        compiler_params=pltpu.CompilerParams(
            collective_id=0, has_side_effects=True, vmem_limit_bytes=40 << 20
        ),
        name="lin_attn_bwd",
    )(
        doc_ids,
        pltpu.with_memory_space_constraint(gain, pltpu.HBM),
        pltpu.with_memory_space_constraint(queries.reshape(flat), pltpu.HBM),
        pltpu.with_memory_space_constraint(keys.reshape(flat), pltpu.HBM),
        pltpu.with_memory_space_constraint(values.reshape(flat), pltpu.HBM),
        pltpu.with_memory_space_constraint(grad_normed.reshape(flat), pltpu.HBM),
    )
    anywhere = pl.BlockSpec(memory_space=pl.ANY)
    gq, gk, gv, gg = pl.pallas_call(
        writer,
        out_shape=(big, big, big, jax.ShapeDtypeStruct((hps, 1, DIM), F32)),
        in_specs=[anywhere] * 4,
        out_specs=(anywhere,) * 4,
        scratch_shapes=[dma((4,))],
        compiler_params=pltpu.CompilerParams(vmem_limit_bytes=1 << 20),
        name="write_out",
    )(gq, gk, gv, gg)
    whole = (batch, length, features)
    return gq.reshape(whole), gk.reshape(whole), gv.reshape(whole), gg.reshape(features // ndp)


def solution(mesh):
    rows = P(("group", "dp"), "ctx", None)
    return jax.shard_map(
        functools.partial(per_device, mesh.shape["ctx"], mesh.shape["dp"]),
        mesh=mesh,
        in_specs=(rows, rows, rows, rows, P(), P(("group", "dp"), "ctx")),
        out_specs=(rows, rows, rows, P(("group", "dp"))),
        check_vma=False,
    )
```

```python
import functools

import jax
import jax.numpy as jnp
from jax import lax
from jax.experimental import pallas as pl
from jax.experimental.pallas import tpu as pltpu
from jax.sharding import PartitionSpec as P

HEADS = 16
DIM = 128
SPAN = 128
SHIFT = 4
GROUP = 4
STAGE = 1
HELD = 4
MESH = pl.DeviceIdType.MESH
F32 = jnp.float32
BF16 = jnp.bfloat16


def dot(a, b, ca, cb):
    return lax.dot_general(a, b, (((ca,), (cb,)), ((), ())), preferred_element_type=F32)


def kernel(
    n, ndp, chain, shift, doc, gain_hbm, q_hbm, k_hbm, v_hbm, y_hbm,
    gq, gk, gv, gg_out,
    gain_in, gain, q, k, v, y, kvb, kvr, intra, attn, da, stb, qdo, bkr, gkp, gvp,
    tag, tagl, tagr, ssq, inn, gsum, ga, gb, stage, rstage, dsq, dnn, stat, statr, scal, scalr,
    in_sem, ks, kr, bs, br, ts, tr, gas, gar, gbs, gbr, ss, sr, ms, mr,
):
    me = lax.axis_index("ctx")
    mydp = lax.axis_index("dp")
    right, left = lax.rem(me + 1, n), lax.rem(me + n - 1, n)
    has_right, has_left = me < n - 1, me > 0
    hps = HEADS // ndp
    plain = HEADS - shift
    features = HEADS * DIM

    loads = [
        pltpu.make_async_copy(src, dst, in_sem.at[i])
        for i, (src, dst) in enumerate(
            ((k_hbm, k), (v_hbm, v), (q_hbm, q), (y_hbm, y), (gain_hbm, gain_in))
        )
    ]
    for load in loads:
        load.start()

    barrier = pltpu.get_barrier_semaphore()
    for o in range(1, n):
        pl.semaphore_signal(barrier, inc=1, device_id={"ctx": lax.rem(me + o, n)}, device_id_type=MESH)
    for o in range(1, ndp):
        pl.semaphore_signal(barrier, inc=1, device_id={"dp": lax.rem(mydp + o, ndp)}, device_id_type=MESH)

    def cols(h):
        return pl.ds(pl.multiple_of(h * DIM, DIM), DIM)

    def loop(first, last, body, group=GROUP):
        whole = (last - first) // group

        def step(g, _):
            body([first + g * group + i for i in range(group)])
            return 0

        if whole == 1:
            step(0, 0)
        elif whole > 1:
            lax.fori_loop(0, whole, step, 0)
        if first + whole * group < last:
            body(list(range(first + whole * group, last)))

    def each(first, last, body):
        def step(h, _):
            body(h)
            return 0

        if last > first:
            lax.fori_loop(first, last, step, 0)

    def remote(src, dst, s, r, where):
        return pltpu.make_async_remote_copy(
            src_ref=src, dst_ref=dst, send_sem=s, recv_sem=r, device_id=where, device_id_type=MESH
        )

    to_right, to_left = {"ctx": right}, {"ctx": left}

    def kv_copy(h):
        return remote(kvb.at[h], kvr.at[h], ks.at[h], kr.at[h], to_right)

    def back_copy(h):
        return remote(qdo.at[h], bkr.at[h], bs.at[h], br.at[h], to_left)

    def stage_copy(j):
        return remote(stage.at[j], rstage.at[j], ss.at[j], sr.at[j], to_left)

    tag_right = remote(tag, tagl, ts.at[0], tr.at[0], to_right)
    tag_left = remote(tag, tagr, ts.at[1], tr.at[1], to_left)
    stat_right = remote(stat, statr, ms.at[0], mr.at[0], to_right)
    scal_left = remote(scal, scalr, ms.at[1], mr.at[1], to_left)

    own = (doc[0, 0] + 1).astype(F32)
    tag[...] = jnp.full((8, 128), own, F32)
    ssq[...] = jnp.zeros_like(ssq)
    inn[...] = jnp.zeros_like(inn)
    dsq[...] = jnp.zeros_like(dsq)
    dnn[...] = jnp.zeros_like(dnn)

    @pl.when(jnp.logical_not(has_left))
    def _():
        tagl[...] = jnp.full((8, 128), -1.0, F32)
        kvr[...] = jnp.zeros_like(kvr)
        statr[...] = jnp.zeros_like(statr)

    @pl.when(jnp.logical_not(has_right))
    def _():
        tagr[...] = jnp.full((8, 128), -1.0, F32)
        bkr[...] = jnp.zeros_like(bkr)

    rows = lax.broadcasted_iota(jnp.int32, (SPAN, SPAN), 0)
    lanes = lax.broadcasted_iota(jnp.int32, (SPAN, SPAN), 1)
    causal = rows >= lanes

    loads[0].wait()
    loads[1].wait()
    pl.semaphore_wait(barrier, n - 1 + ndp - 1)

    @pl.when(has_right)
    def _():
        tag_right.start()

    @pl.when(has_left)
    def _():
        tag_left.start()

    def kv_only(hs):
        for h, m in [(h, dot(k[:, cols(h)], v[:, cols(h)], 0, 0)) for h in hs]:
            kvb[h] = m

    def kv_step(hs):
        kv_only(hs)
        if not chain:

            @pl.when(has_right)
            def _():
                for h in hs:
                    kv_copy(h).start()

    def local_step(hs):
        scores = [dot(q[:, cols(h)], k[:, cols(h)], 1, 1) for h in hs]
        ws = [jnp.where(causal, x, 0.0).astype(BF16) for x in scores]
        outs = [dot(w, v[:, cols(h)], 1, 0) for h, w in zip(hs, ws)]
        for h, w, a in zip(hs, ws, outs):
            intra[:, cols(h)] = w
            attn[:, cols(h)] = a
        return outs

    def sums(terms):
        total = terms[0]
        for term in terms[1:]:
            total = total + term
        return total

    def norm_sums(hs, outs):
        ssq[...] += sums([a * a for a in outs])
        inn[...] += sums([y[:, cols(h)].astype(F32) * gain[h] * a for h, a in zip(hs, outs)])

    def stage_step(js):
        hs = [plain + j for j in js]
        outs = local_step(hs)
        for j, h, a in zip(js, hs, outs):
            stage[j, 0] = q[:, cols(h)].astype(F32)
            stage[j, 1] = y[:, cols(h)].astype(F32)
            stage[j, 2] = a

        @pl.when(has_left)
        def _():
            for j in js:
                stage_copy(j).start()

        norm_sums(hs, outs)

    ahead = min(GROUP, plain)
    loop(0, ahead, kv_step)
    for load in loads[2:]:
        load.wait()
    for h in range(HEADS):
        gain[h] = gain_in[h * DIM : (h + 1) * DIM].astype(F32).reshape(1, DIM)
    loop(0, shift, stage_step, STAGE)
    loop(ahead, plain, kv_step)
    loop(plain, HEADS, kv_only)
    loop(0, plain, local_step)

    @pl.when(has_left)
    def _():
        tag_right.wait_recv()

    @pl.when(has_right)
    def _():
        tag_left.wait_recv()

    from_left = jnp.broadcast_to(tagl[0:1, :] == tag[0:1, :], (DIM, DIM))
    from_right = jnp.broadcast_to(tagr[0:1, :] == tag[0:1, :], (DIM, DIM))

    def state_step(hs):
        @pl.when(has_left)
        def _():
            for h in hs:
                kv_copy(h).wait_recv()

        states = [jnp.where(from_left, kvr[h], 0.0) for h in hs]
        if chain:
            for h, state in zip(hs, states):
                kvb[h] = kvb[h] + state

            @pl.when(has_right)
            def _():
                for h in hs:
                    kv_copy(h).start()

        rounded = [state.astype(BF16) for state in states]
        outs = [attn[:, cols(h)] + dot(q[:, cols(h)], sb, 1, 0) for h, sb in zip(hs, rounded)]
        for h, sb, a in zip(hs, rounded, outs):
            stb[h] = sb
            attn[:, cols(h)] = a
        return outs

    def attn_step(hs):
        norm_sums(hs, state_step(hs))

    def helper_step(js):
        for j in js:
            stage_copy(j).wait_recv()
        kbs = [jnp.where(from_right, kvb[plain + j], 0.0).astype(BF16) for j in js]
        xs = [dot(rstage[j, 0].astype(BF16), kb, 1, 0) for j, kb in zip(js, kbs)]
        olds = [rstage[j, 2] for j in js]
        dsq[...] += sums([(2.0 * a + x) * x for a, x in zip(olds, xs)])
        dnn[...] += sums([rstage[j, 1] * gain[plain + j] * x for j, x in zip(js, xs)])
        for j, a, x in zip(js, olds, xs):
            rstage[j, 2] = a + x

    if shift:
        parts = shift
        for p in range(parts):
            loop(plain * p // parts, plain * (p + 1) // parts, attn_step, 3)

            @pl.when(has_right)
            def _():
                helper_step(list(range(shift * p // parts, shift * (p + 1) // parts)))

        @pl.when(has_right)
        def _():
            stat[0] = jnp.sum(jnp.transpose(dsq[...]).reshape(16, 8, SPAN), axis=0)
            stat[1] = jnp.sum(jnp.transpose(dnn[...]).reshape(16, 8, SPAN), axis=0)
            stat_right.start()

            for j in range(shift):
                kv_copy(plain + j).start()

        @pl.when(has_left)
        def _():
            stat_right.wait_recv()

        extra_sq = jnp.transpose(jnp.broadcast_to(jnp.sum(statr[0], axis=0, keepdims=True), (DIM, SPAN)))
        extra_in = jnp.transpose(jnp.broadcast_to(jnp.sum(statr[1], axis=0, keepdims=True), (DIM, SPAN)))
    else:
        loop(0, HEADS, attn_step)
        extra_sq = extra_in = 0.0

    mean = jnp.broadcast_to(jnp.sum(ssq[...], axis=-1, keepdims=True), (SPAN, DIM)) + extra_sq
    inner = jnp.broadcast_to(jnp.sum(inn[...], axis=-1, keepdims=True), (SPAN, DIM)) + extra_in
    inv = 1.0 / jnp.sqrt(mean / features + 1e-05)
    coef = inner * inv**3 / features

    if shift:
        scal[0] = jnp.transpose(inv)[0:8]
        scal[1] = jnp.transpose(coef)[0:8]

        @pl.when(has_left)
        def _():
            scal_left.start()

    def da_step(hs):
        ds = []
        for h in hs:
            a = attn[:, cols(h)]
            g = y[:, cols(h)].astype(F32)
            ds.append((g * gain[h] * inv - a * coef).astype(BF16))
        for h, d in zip(hs, ds):
            da[:, cols(h)] = d
        return ds

    def gain_step(hs):
        rows_of = [
            jnp.sum(y[:, cols(h)].astype(F32) * attn[:, cols(h)] * inv, axis=0, keepdims=True) for h in hs
        ]
        for h, row in zip(hs, rows_of):
            gsum[h] = row

    def held_step(hs):
        for h, m in [(h, dot(q[:, cols(h)], d, 0, 0)) for h, d in zip(hs, da_step(hs))]:
            qdo[h] = m

    def send_step(hs):
        held_step(hs)
        if not chain:

            @pl.when(has_left)
            def _():
                for h in hs:
                    back_copy(h).start()

    def grad_step(hs):
        ds = [da[:, cols(h)] for h in hs]
        scores = [dot(d, v[:, cols(h)], 1, 1) for h, d in zip(hs, ds)]
        ws = [jnp.where(causal, x, 0.0).astype(BF16) for x in scores]
        far = [dot(d, stb[h], 1, 1) for h, d in zip(hs, ds)]
        vs = [dot(intra[:, cols(h)], d, 0, 0) for h, d in zip(hs, ds)]
        qs = [dot(w, k[:, cols(h)], 1, 0) + f for h, w, f in zip(hs, ws, far)]
        kk = [dot(w, q[:, cols(h)], 0, 0) for h, w in zip(hs, ws)]
        for h, a, b, c in zip(hs, qs, kk, vs):
            gq[:, cols(h)] = a.astype(BF16)
            gkp[:, cols(h)] = b
            gvp[:, cols(h)] = c
        gain_step(hs)

    sent = plain - HELD if shift else plain
    loop(0, sent, send_step, 2)
    loop(sent, plain, held_step)

    def late_step(hs):
        state_step(hs)
        da_step(hs)

    if shift:
        loop(0, plain, grad_step)
        loop(plain, HEADS, late_step)

    def ga_copy(o):
        to = lax.rem(mydp + o, ndp)
        return remote(
            gsum.at[pl.ds(to * hps, hps)], ga.at[o - 1], gas.at[o - 1], gar.at[o - 1], {"dp": to}
        )

    loop(plain if shift else 0, HEADS, grad_step)
    for o in range(1, ndp):
        ga_copy(o).start()

    def finish(hs, backs):
        rounded = [back.astype(BF16) for back in backs]
        kk = [gkp[:, cols(h)] + dot(v[:, cols(h)], bb, 1, 1) for h, bb in zip(hs, rounded)]
        vs = [gvp[:, cols(h)] + dot(k[:, cols(h)], bb, 1, 0) for h, bb in zip(hs, rounded)]
        for h, a, b in zip(hs, kk, vs):
            gk[:, cols(h)] = a.astype(BF16)
            gv[:, cols(h)] = b.astype(BF16)

    if shift:

        @pl.when(has_right)
        def _():
            scal_left.wait_recv()
            r_inv = jnp.transpose(jnp.broadcast_to(scalr[0, 0:1], (DIM, SPAN)))
            r_coef = jnp.transpose(jnp.broadcast_to(scalr[1, 0:1], (DIM, SPAN)))

            def near(js):
                ds = [
                    (rstage[j, 1] * gain[plain + j] * r_inv - rstage[j, 2] * r_coef).astype(BF16) for j in js
                ]
                for j, m in [(j, dot(rstage[j, 0].astype(BF16), d, 0, 0)) for j, d in zip(js, ds)]:
                    bkr[plain + j] = m

            loop(0, shift, near)

    for o in range(1, ndp):
        ga_copy(o).wait_recv()
    mine = gsum[pl.ds(mydp * hps, hps)]
    for o in range(1, ndp):
        mine = mine + ga[o - 1]
    gb[me] = mine

    def gb_send(o):
        return remote(gb.at[me], gb.at[me], gbs.at[o - 1], gbr.at[o - 1], {"ctx": lax.rem(me + o, n)})

    def gb_recv(o):
        source = lax.rem(me + n - o, n)
        return remote(gb.at[source], gb.at[source], gbs.at[o - 1], gbr.at[o - 1], {"ctx": lax.rem(me + o, n)})

    for o in range(1, n):
        gb_send(o).start()

    if shift:

        @pl.when(has_left)
        def _():
            for h in range(sent, plain):
                back_copy(h).start()

        def near_finish(hs):
            finish(hs, [jnp.where(from_right, bkr[h], 0.0) for h in hs])

        loop(plain, HEADS, near_finish)

    def back_step(hs):
        @pl.when(has_right)
        def _():
            for h in hs:
                back_copy(h).wait_recv()

        backs = [jnp.where(from_right, bkr[h], 0.0) for h in hs]
        if chain:
            for h, back in zip(hs, backs):
                qdo[h] = qdo[h] + back

            @pl.when(has_left)
            def _():
                for h in hs:
                    back_copy(h).start()

        finish(hs, backs)

    loop(0, plain, back_step, 2)

    for o in range(1, n):
        gb_recv(o).wait_recv()
    total = gb[0]
    for i in range(1, n):
        total = total + gb[i]
    gg_out[...] = total

    for o in range(1, n):
        gb_send(o).wait_send()
    for o in range(1, ndp):
        ga_copy(o).wait_send()

    @pl.when(has_right)
    def _():
        tag_right.wait_send()
        each(0, HEADS, lambda h: kv_copy(h).wait_send())
        if shift:
            stat_right.wait_send()

    @pl.when(has_left)
    def _():
        tag_left.wait_send()
        each(0, plain, lambda h: back_copy(h).wait_send())
        if shift:
            each(0, shift, lambda j: stage_copy(j).wait_send())
            scal_left.wait_send()


def writer(*refs):
    ins, outs, sem = refs[:4], refs[4:8], refs[8]
    copies = [pltpu.make_async_copy(a, b, sem.at[i]) for i, (a, b) in enumerate(zip(ins, outs))]
    for copy in copies:
        copy.start()
    for copy in copies:
        copy.wait()


def per_device(n, ndp, queries, keys, values, grad_normed, gain, doc_ids):
    batch, length, features = queries.shape
    flat = (length, features)
    hps = HEADS // ndp
    chain = n // 2 > 2
    shift = 0 if chain else SHIFT
    spare = max(shift, 1)
    vmem = pltpu.VMEM
    dma = pltpu.SemaphoreType.DMA
    hbm = pl.BlockSpec(memory_space=pltpu.HBM)
    near = pl.BlockSpec(memory_space=pltpu.VMEM)
    big = jax.ShapeDtypeStruct(flat, BF16)
    square = (HEADS, DIM, DIM)
    small = (2, 8, DIM)
    gq, gk, gv, gg = pl.pallas_call(
        functools.partial(kernel, n, ndp, chain, shift),
        out_shape=(big, big, big, jax.ShapeDtypeStruct((hps, 1, DIM), F32)),
        in_specs=[pl.BlockSpec(memory_space=pltpu.SMEM), hbm, hbm, hbm, hbm, hbm],
        out_specs=(near, near, near, near),
        scratch_shapes=[
            vmem((features,), BF16), vmem((HEADS, 1, DIM), F32),
            vmem(flat, BF16), vmem(flat, BF16), vmem(flat, BF16), vmem(flat, BF16),
            vmem(square, F32), vmem(square, F32),
            vmem(flat, BF16), vmem(flat, F32), vmem(flat, BF16), vmem(square, BF16),
            vmem(square, F32), vmem(square, F32),
            vmem(flat, F32), vmem(flat, F32),
            vmem((8, DIM), F32), vmem((8, DIM), F32), vmem((8, DIM), F32),
            vmem((SPAN, DIM), F32), vmem((SPAN, DIM), F32),
            vmem((HEADS, 1, DIM), F32), vmem((ndp - 1, hps, 1, DIM), F32), vmem((n, hps, 1, DIM), F32),
            vmem((spare, 3, SPAN, DIM), F32), vmem((spare, 3, SPAN, DIM), F32),
            vmem((SPAN, DIM), F32), vmem((SPAN, DIM), F32),
            vmem(small, F32), vmem(small, F32), vmem(small, F32), vmem(small, F32),
            dma((5,)),
            dma((HEADS,)), dma((HEADS,)), dma((HEADS,)), dma((HEADS,)),
            dma((2,)), dma((2,)),
            dma((ndp - 1,)), dma((ndp - 1,)), dma((n - 1,)), dma((n - 1,)),
            dma((spare,)), dma((spare,)), dma((2,)), dma((2,)),
        ],
        compiler_params=pltpu.CompilerParams(
            collective_id=0, has_side_effects=True, vmem_limit_bytes=40 << 20
        ),
        name="lin_attn_bwd",
    )(
        doc_ids,
        pltpu.with_memory_space_constraint(gain, pltpu.HBM),
        pltpu.with_memory_space_constraint(queries.reshape(flat), pltpu.HBM),
        pltpu.with_memory_space_constraint(keys.reshape(flat), pltpu.HBM),
        pltpu.with_memory_space_constraint(values.reshape(flat), pltpu.HBM),
        pltpu.with_memory_space_constraint(grad_normed.reshape(flat), pltpu.HBM),
    )
    anywhere = pl.BlockSpec(memory_space=pl.ANY)
    gq, gk, gv, gg = pl.pallas_call(
        writer,
        out_shape=(big, big, big, jax.ShapeDtypeStruct((hps, 1, DIM), F32)),
        in_specs=[anywhere] * 4,
        out_specs=(anywhere,) * 4,
        scratch_shapes=[dma((4,))],
        compiler_params=pltpu.CompilerParams(vmem_limit_bytes=1 << 20),
        name="write_out",
    )(gq, gk, gv, gg)
    whole = (batch, length, features)
    return gq.reshape(whole), gk.reshape(whole), gv.reshape(whole), gg.reshape(features // ndp)


def solution(mesh):
    rows = P(("group", "dp"), "ctx", None)
    return jax.shard_map(
        functools.partial(per_device, mesh.shape["ctx"], mesh.shape["dp"]),
        mesh=mesh,
        in_specs=(rows, rows, rows, rows, P(), P(("group", "dp"), "ctx")),
        out_specs=(rows, rows, rows, P(("group", "dp"))),
        check_vma=False,
    )
```
